512 devices in a mesh: ctx: 128 (over x_hi, y, z), tensor: 4 (over x_lo, core).
Axes of the slice: x: 4 (x_hi: 2, x_lo: 2; x = x_hi * 2 + x_lo), y: 8, z: 8, core: 2. Of those that a mesh axis runs over, the one named last changes fastest.
Arguments:
- queries: bfloat16 [65536, 4096], P(('ctx', 'tensor')), may hold values from -6 to 6
- keys: bfloat16 [65536, 1024], P(('ctx', 'tensor')), may hold values from -10 to 10
- values: bfloat16 [65536, 1024], P(('ctx', 'tensor')), may hold values from -6 to 6
- mid_offsets: int32 [8], P('tensor'), may hold values from 0 to 7
- far_offsets: int32 [8], P('tensor'), may hold values from 0 to 63
Outputs:
- attended: bfloat16 [65536, 4096], P(('ctx', 'tensor'))
The draws below stay inside these ranges and needn't reach their ends.
All inputs are finite; a program needn't handle non-finite values.
Results may differ from the reference program's by a relative error of at most 0.003.
Values may be sent and summed in bfloat16 or wider, within the bound.
A program may use at most 64 MiB of HBM per device.

```python
import jax
import jax.numpy as jnp
from jax import lax

HEADS = 32
KV_HEADS = 8
HEAD_DIM = 128
RATE_MID = 8
RATE_FAR = 64
TOKENS = 65536
NEAR_SEG = 512
MID_SEG = 8192


def drawn_pair(key):
    query_vals = jnp.clip(jax.random.normal(jax.random.fold_in(key, 11), (TOKENS, HEADS, HEAD_DIM), jnp.float32), -6.0, 6.0)
    key_vals = 2.5 * jnp.clip(jax.random.normal(jax.random.fold_in(key, 12), (TOKENS, KV_HEADS, HEAD_DIM), jnp.float32), -4.0, 4.0)
    return (query_vals.reshape(TOKENS, HEADS * HEAD_DIM), key_vals.reshape(TOKENS, KV_HEADS * HEAD_DIM))


def draw_queries(key, part):
    return drawn_pair(key)[0].astype(jnp.bfloat16)


def draw_keys(key, part):
    return drawn_pair(key)[1].astype(jnp.bfloat16)


def set_ends(array, own_key, least, largest):
    extent = array.shape
    index_at = [jax.random.randint(jax.random.fold_in(own_key, axis), (), 0, extent[axis]) for axis in range(len(extent))]
    array = array.at[tuple(index_at)].set(least)
    longest = extent.index(max(extent))
    index_at[longest] = (index_at[longest] + 1) % extent[longest]
    return array.at[tuple(index_at)].set(largest)


def block_scale(stream_key, dims, shards, smallest, high):
    def one(dim, blocks):
        steps = jax.random.uniform(jax.random.fold_in(jax.random.fold_in(stream_key, 6), dim), (blocks,), jnp.float32, smallest / len(shards), high / len(shards))
        return jnp.repeat(jnp.exp(steps), dims[dim] // blocks).reshape((-1,) + (1,) * (len(dims) - dim - 1))

    gain = one(*shards[0])
    for cut in shards[1:]:
        gain = gain * one(*cut)
    return gain


def bell_draw(rng, shape, spread, limit, cuts=(), kind=jnp.bfloat16):
    level = block_scale(rng, shape, cuts, -0.22, 0.18) if cuts else 1.0
    entries = jax.random.normal(rng, shape, jnp.float32) * spread * level
    return jnp.minimum(jnp.maximum(entries, -limit), limit).astype(kind)


def setup_inputs(seed: int = 0) -> dict:
    arg_keys = jax.random.split(jax.random.key(seed), 6)
    queries = draw_queries(jax.random.fold_in(arg_keys[5], 71), 0)
    keys = draw_keys(jax.random.fold_in(arg_keys[5], 71), 0)
    values = bell_draw(arg_keys[2], (TOKENS, KV_HEADS * HEAD_DIM), 1.0, 6.0, ((0, 512),))
    mid_offsets = set_ends(jax.random.randint(arg_keys[3], (KV_HEADS,), 0, RATE_MID), jax.random.fold_in(arg_keys[3], 1), 0, RATE_MID - 1).astype(jnp.int32)
    far_offsets = set_ends(jax.random.randint(arg_keys[4], (KV_HEADS,), 0, RATE_FAR), jax.random.fold_in(arg_keys[4], 1), 0, RATE_FAR - 1).astype(jnp.int32)
    return {"queries": queries, "keys": keys, "values": values, "mid_offsets": mid_offsets, "far_offsets": far_offsets}


NEG_FILL = -1.0e30


def head_stats(query_rows, key_rows, value_rows, allowed, scale_factor):
    scores = jnp.einsum("agd,bd->agb", query_rows.astype(jnp.float32), key_rows.astype(jnp.float32)) * scale_factor
    scores = jnp.where(allowed[:, None, :], scores, NEG_FILL)
    maxima = jnp.max(scores, axis=-1)
    powers = jnp.exp(scores - maxima[..., None])
    totals = jnp.sum(powers, axis=-1)
    weights = powers.astype(jnp.bfloat16)
    weighted = jnp.einsum("agb,bd->agd", weights.astype(jnp.float32), value_rows.astype(jnp.float32))
    return maxima, totals, weighted


def blocked(query_rows, key_rows, value_rows, seg_len, scale_factor):
    row_count = query_rows.shape[0]
    blocks = row_count // seg_len
    per_group = query_rows.shape[1]
    allowed = jnp.arange(seg_len)[:, None] >= jnp.arange(seg_len)[None, :]

    def one_block(items):
        return head_stats(items[0], items[1], items[2], allowed, scale_factor)

    maxima, totals, weighted = lax.map(one_block, (
        query_rows.reshape(blocks, seg_len, per_group, HEAD_DIM),
        key_rows.reshape(blocks, seg_len, HEAD_DIM),
        value_rows.reshape(blocks, seg_len, HEAD_DIM)))
    return (maxima.reshape(row_count, per_group), totals.reshape(row_count, per_group),
            weighted.reshape(row_count, per_group, HEAD_DIM))


def windowed(query_rows, key_rows, value_rows, scale_factor):
    blocks = TOKENS // NEAR_SEG
    per_group = query_rows.shape[1]
    key_blocks = key_rows.reshape(blocks, NEAR_SEG, HEAD_DIM)
    value_blocks = value_rows.reshape(blocks, NEAR_SEG, HEAD_DIM)
    zero_block = jnp.zeros((1, NEAR_SEG, HEAD_DIM), key_rows.dtype)
    key_pairs = jnp.concatenate([jnp.concatenate([zero_block, key_blocks[:-1]], 0), key_blocks], 1)
    value_pairs = jnp.concatenate([jnp.concatenate([zero_block, value_blocks[:-1]], 0), value_blocks], 1)
    query_index = jnp.arange(NEAR_SEG)[:, None]
    key_index = jnp.arange(2 * NEAR_SEG)[None, :]

    def one_block(items):
        block_number = items[3]
        allowed = jnp.where(key_index >= NEAR_SEG, key_index - NEAR_SEG <= query_index,
                            (key_index > query_index) & (block_number > 0))
        return head_stats(items[0], items[1], items[2], allowed, scale_factor)

    maxima, totals, weighted = lax.map(one_block, (
        query_rows.reshape(blocks, NEAR_SEG, per_group, HEAD_DIM), key_pairs, value_pairs,
        jnp.arange(blocks, dtype=jnp.int32)))
    return (maxima.reshape(TOKENS, per_group), totals.reshape(TOKENS, per_group),
            weighted.reshape(TOKENS, per_group, HEAD_DIM))


def dilated(query_rows, key_rows, value_rows, offset, rate, seg_rows, scale_factor):
    per_group = query_rows.shape[1]
    offset = offset.astype(jnp.int32)
    picked_q = lax.dynamic_index_in_dim(query_rows.reshape(TOKENS // rate, rate, per_group, HEAD_DIM), offset, 1, False)
    picked_k = lax.dynamic_index_in_dim(key_rows.reshape(TOKENS // rate, rate, HEAD_DIM), offset, 1, False)
    picked_v = lax.dynamic_index_in_dim(value_rows.reshape(TOKENS // rate, rate, HEAD_DIM), offset, 1, False)
    maxima, totals, weighted = blocked(picked_q, picked_k, picked_v, seg_rows, scale_factor)
    chosen = jnp.arange(rate, dtype=jnp.int32) == offset
    maxima = jnp.where(chosen[None, :, None], maxima[:, None, :], NEG_FILL).reshape(TOKENS, per_group)
    totals = jnp.where(chosen[None, :, None], totals[:, None, :], jnp.float32(0.0)).reshape(TOKENS, per_group)
    weighted = jnp.where(chosen[None, :, None, None], weighted[:, None], jnp.float32(0.0)).reshape(TOKENS, per_group, HEAD_DIM)
    return maxima, totals, weighted


def reference(queries, keys, values, mid_offsets, far_offsets):
    per_group = HEADS // KV_HEADS
    scale_factor = HEAD_DIM ** -0.5
    query_heads = queries.reshape(TOKENS, KV_HEADS, per_group, HEAD_DIM).transpose(1, 0, 2, 3)
    key_heads = keys.reshape(TOKENS, KV_HEADS, HEAD_DIM).transpose(1, 0, 2)
    value_heads = values.reshape(TOKENS, KV_HEADS, HEAD_DIM).transpose(1, 0, 2)

    def one_head(items):
        query_rows, key_rows, value_rows, mid_off, far_off = items
        near_stats = windowed(query_rows, key_rows, value_rows, scale_factor)
        mid_stats = dilated(query_rows, key_rows, value_rows, mid_off, RATE_MID, MID_SEG // RATE_MID, scale_factor)
        far_stats = dilated(query_rows, key_rows, value_rows, far_off, RATE_FAR, TOKENS // RATE_FAR, scale_factor)
        highest = jnp.maximum(jnp.maximum(near_stats[0], mid_stats[0]), far_stats[0])
        denominator = jnp.zeros_like(highest)
        numerator = jnp.zeros((TOKENS, per_group, HEAD_DIM), jnp.float32)
        for branch_stats in (near_stats, mid_stats, far_stats):
            factor = jnp.exp(branch_stats[0] - highest)
            denominator = denominator + factor * branch_stats[1]
            numerator = numerator + factor[..., None] * branch_stats[2]
        return (numerator / denominator[..., None]).astype(jnp.bfloat16)

    result = lax.map(one_head, (query_heads, key_heads, value_heads, mid_offsets, far_offsets))
    return result.transpose(1, 0, 2, 3).reshape(TOKENS, HEADS * HEAD_DIM)
```

```python
import jax
import jax.numpy as jnp
from jax import lax
from jax.experimental import pallas as pl
from jax.experimental.pallas import tpu as pltpu
from jax.sharding import PartitionSpec as P

HEADS = 32
KV_HEADS = 8
HEAD_DIM = 128
RATE_MID = 8
RATE_FAR = 64


NEG_FILL = -1e30


RING = 8
MESH_IDS = pl.DeviceIdType.MESH


def exchange_body(
    kv_ref, mid_ref, fk_ref, fv_ref,
    prev_out, mid_out, fk_out, fv_out,
    local_sem, prev_sem, x_send, x_recv, mid_send, mid_recv, fwd_send, fwd_recv,
    k1_send, k1_recv, v1_send, v1_recv, k2_send, k2_recv, v2_send, v2_recv,
):
    place = lax.axis_index("ctx")
    total = 2 * RING * RING
    z = lax.rem(place, RING)
    y = lax.rem(place // RING, RING)
    x = place // (RING * RING)

    def at(xi, yi, zi):
        return {"ctx": (xi * RING + yi) * RING + zi}

    def z_peer(step):
        return at(x, y, lax.rem(z + step, RING))

    def y_peer(step):
        return at(x, lax.rem(y + step, RING), z)

    x_peer = at(1 - x, y, z)
    parity = lax.rem(y, 2)
    y_pair = at(x, y + 1 - 2 * parity, z)
    after = {"ctx": lax.rem(place + 1, total)}
    before = {"ctx": lax.rem(place + total - 1, total)}

    barrier = pltpu.get_barrier_semaphore()
    greeted = [x_peer, after, before]
    greeted += [z_peer(step) for step in range(1, RING)]
    greeted += [y_peer(step) for step in range(1, RING)]
    for peer in greeted:
        pl.semaphore_signal(barrier, inc=1, device_id=peer, device_id_type=MESH_IDS)
    pl.semaphore_wait(barrier, len(greeted))

    def remote(source, target, send, recv, peer):
        copy = pltpu.make_async_remote_copy(
            src_ref=source, dst_ref=target, send_sem=send, recv_sem=recv,
            device_id=peer, device_id_type=MESH_IDS,
        )
        copy.start()
        return copy

    own_k = pltpu.make_async_copy(fk_ref, fk_out.at[y, z, x], local_sem.at[0])
    own_v = pltpu.make_async_copy(fv_ref, fv_out.at[z, y, x], local_sem.at[1])
    own_mid = pltpu.make_async_copy(mid_ref, mid_out.at[parity, z], local_sem.at[2])
    own_k.start()
    own_v.start()
    own_mid.start()
    x_k = remote(fk_ref, fk_out.at[y, z, x], x_send.at[0], x_recv.at[0], x_peer)
    x_v = remote(fv_ref, fv_out.at[z, y, x], x_send.at[1], x_recv.at[1], x_peer)
    order = [4, 3, 5, 2, 6, 1, 7]
    mids = {
        step: remote(
            mid_ref, mid_out.at[parity, z], mid_send.at[step], mid_recv.at[step], z_peer(step)
        )
        for step in order
    }
    forwards = [
        remote(mid_ref, mid_out.at[parity, z], fwd_send.at[0], fwd_recv.at[0], y_pair)
    ]
    own_k.wait()
    own_v.wait()
    x_k.wait_recv()
    x_v.wait_recv()
    firsts_k = {
        step: remote(
            fk_out.at[y, z], fk_out.at[y, z], k1_send.at[step], k1_recv.at[step], z_peer(step)
        )
        for step in order
    }
    firsts_v = {
        step: remote(
            fv_out.at[z, y], fv_out.at[z, y], v1_send.at[step], v1_recv.at[step], y_peer(step)
        )
        for step in order
    }
    ahead = remote(kv_ref, prev_out, prev_sem.at[0], prev_sem.at[1], after)
    for step in order:
        firsts_v[step].wait_recv()
    seconds_v = {
        step: remote(fv_out.at[z], fv_out.at[z], v2_send.at[step], v2_recv.at[step], z_peer(step))
        for step in order
    }
    for step in order:
        firsts_k[step].wait_recv()
    seconds_k = {
        step: remote(fk_out.at[y], fk_out.at[y], k2_send.at[step], k2_recv.at[step], y_peer(step))
        for step in order
    }
    for step in [1, 7, 2, 6, 3, 5, 4]:
        mids[step].wait_recv()
        source = lax.rem(z + RING - step, RING)
        forwards.append(
            remote(
                mid_out.at[parity, source], mid_out.at[parity, source],
                fwd_send.at[step], fwd_recv.at[step], y_pair,
            )
        )
    for copy in forwards:
        copy.wait_recv()
    for step in order:
        seconds_k[step].wait_recv()
        seconds_v[step].wait_recv()
    ahead.wait()
    own_mid.wait()
    x_k.wait_send()
    x_v.wait_send()
    for step in order:
        for group in (mids, firsts_k, firsts_v, seconds_k, seconds_v):
            group[step].wait_send()
    for copy in forwards:
        copy.wait_send()


def exchange(kv_rows, mid_kv, far_k, far_v):
    sems = [pltpu.SemaphoreType.DMA((RING,)) for _ in range(12)]
    return pl.pallas_call(
        exchange_body,
        out_shape=[
            jax.ShapeDtypeStruct(kv_rows.shape, jnp.bfloat16),
            jax.ShapeDtypeStruct((2, RING) + mid_kv.shape, jnp.bfloat16),
            jax.ShapeDtypeStruct((RING, RING, 2) + far_k.shape, jnp.bfloat16),
            jax.ShapeDtypeStruct((RING, RING, 2) + far_v.shape, jnp.bfloat16),
        ],
        in_specs=[pl.BlockSpec(memory_space=pltpu.VMEM)] * 4,
        out_specs=[pl.BlockSpec(memory_space=pltpu.VMEM)] * 4,
        scratch_shapes=[
            pltpu.SemaphoreType.DMA((3,)),
            pltpu.SemaphoreType.DMA((2,)),
            pltpu.SemaphoreType.DMA((2,)),
            pltpu.SemaphoreType.DMA((2,)),
        ]
        + sems,
        compiler_params=pltpu.CompilerParams(collective_id=0, has_side_effects=True),
        name="exchange",
    )(kv_rows, mid_kv, far_k, far_v)


def head_stats(query_rows, key_rows, value_rows, allowed, scale_factor):
    scores = (
        jnp.einsum("agd,bd->agb", query_rows, key_rows, preferred_element_type=jnp.float32)
        * scale_factor
    )
    scores = jnp.where(allowed[:, None, :], scores, NEG_FILL)
    maxima = jnp.max(scores, axis=-1)
    powers = jnp.exp(scores - maxima[..., None])
    totals = jnp.sum(powers, axis=-1)
    weights = powers.astype(jnp.bfloat16)
    weighted = jnp.einsum("agb,bd->agd", weights, value_rows, preferred_element_type=jnp.float32)
    return (maxima, totals, weighted)


def branch_stats(query_rows, kv_rows, allowed, scale_factor):
    query_heads = query_rows.transpose(1, 0, 2, 3)
    key_heads = kv_rows[:, 0].transpose(1, 0, 2)
    value_heads = kv_rows[:, 1].transpose(1, 0, 2)

    def one_head(items):
        return head_stats(items[0], items[1], items[2], allowed, scale_factor)

    return lax.map(one_head, (query_heads, key_heads, value_heads))


def pick_rows(rows, offsets, rate, kv_dim):
    shaped = rows.reshape((rows.shape[0] // rate, rate) + rows.shape[1:])
    chosen = jnp.arange(rate, dtype=jnp.int32)[:, None] == offsets[None, :]
    hit_shape = [1] * shaped.ndim
    hit_shape[1] = rate
    hit_shape[kv_dim + 1] = offsets.shape[0]
    kept = jnp.where(chosen.reshape(hit_shape), shaped, jnp.zeros((), rows.dtype))
    return jnp.sum(kept, axis=1)


def spread_stats(stats, offsets, rate):
    maxima, totals, weighted = stats
    kv_local = maxima.shape[0]
    per_group = maxima.shape[2]
    chosen = jnp.arange(rate, dtype=jnp.int32)[None, :] == offsets[:, None]
    maxima = jnp.where(chosen[:, None, :, None], maxima[:, :, None, :], NEG_FILL).reshape(
        kv_local, -1, per_group
    )
    totals = jnp.where(chosen[:, None, :, None], totals[:, :, None, :], jnp.float32(0.0)).reshape(
        kv_local, -1, per_group
    )
    weighted = jnp.where(chosen[:, None, :, None, None], weighted[:, :, None], jnp.float32(0.0))
    return (maxima, totals, weighted.reshape(kv_local, -1, per_group, weighted.shape[-1]))


def on_device(queries, keys, values, mid_offsets, far_offsets):
    count = lax.axis_size("tensor")
    own = queries.shape[0]
    kv_rows = jnp.concatenate(
        [keys.reshape(own, count, -1), values.reshape(own, count, -1)], axis=2
    ).reshape(own, -1)
    kv_rows = lax.all_to_all(kv_rows, "tensor", split_axis=1, concat_axis=0, tiled=True)
    queries = lax.all_to_all(queries, "tensor", split_axis=1, concat_axis=0, tiled=True)
    tok_rows = queries.shape[0]
    kv_local = mid_offsets.shape[0]
    per_group = HEADS // KV_HEADS
    scale_factor = HEAD_DIM ** (-0.5)
    query_rows = queries.reshape(tok_rows, kv_local, per_group, HEAD_DIM)
    ctx_count = lax.axis_size("ctx")
    ctx_place = lax.axis_index("ctx")
    team_size = min(16, ctx_count)
    kv_dims = (2, kv_local, HEAD_DIM)
    kv_heads = kv_rows.reshape((tok_rows,) + kv_dims)
    mid_kv = pick_rows(kv_heads, mid_offsets, RATE_MID, 2)
    far_kv = pick_rows(kv_heads, far_offsets, RATE_FAR, 2)
    mid_count = tok_rows // RATE_MID
    far_count = tok_rows // RATE_FAR
    far_flat = far_kv.transpose(1, 2, 0, 3).reshape(2, kv_local * far_count, HEAD_DIM)
    previous, mid_all, far_k, far_v = exchange(
        kv_rows, mid_kv.reshape(mid_count, -1), far_flat[0], far_flat[1]
    )
    mid_all = mid_all.reshape((team_size * mid_count,) + kv_dims)
    far_split = (RING, RING, 2, kv_local, far_count, HEAD_DIM)
    far_k = far_k.reshape(far_split).transpose(3, 2, 0, 1, 4, 5)
    far_v = far_v.reshape(far_split).transpose(3, 2, 1, 0, 4, 5)
    far_all = jnp.stack(
        [far_k.reshape(kv_local, -1, HEAD_DIM), far_v.reshape(kv_local, -1, HEAD_DIM)]
    ).transpose(2, 0, 1, 3)
    near_keys = jnp.concatenate([previous, kv_rows], 0).reshape((-1,) + kv_dims)
    query_index = jnp.arange(tok_rows)[:, None]
    key_index = jnp.arange(2 * tok_rows)[None, :]
    near_allowed = jnp.where(
        key_index >= tok_rows,
        key_index - tok_rows <= query_index,
        (key_index > query_index) & (ctx_place > 0),
    )
    near_stats = branch_stats(query_rows, near_keys, near_allowed, scale_factor)
    mid_queries = pick_rows(query_rows, mid_offsets, RATE_MID, 1)
    far_queries = pick_rows(query_rows, far_offsets, RATE_FAR, 1)
    mid_position = ctx_place % team_size * mid_count + jnp.arange(mid_count)[:, None]
    mid_allowed = jnp.arange(team_size * mid_count)[None, :] <= mid_position
    mid_stats = spread_stats(
        branch_stats(mid_queries, mid_all, mid_allowed, scale_factor), mid_offsets, RATE_MID
    )
    far_position = ctx_place * far_count + jnp.arange(far_count)[:, None]
    far_allowed = jnp.arange(ctx_count * far_count)[None, :] <= far_position
    far_stats = spread_stats(
        branch_stats(far_queries, far_all, far_allowed, scale_factor), far_offsets, RATE_FAR
    )
    highest = jnp.maximum(jnp.maximum(near_stats[0], mid_stats[0]), far_stats[0])
    denominator = jnp.zeros_like(highest)
    numerator = jnp.zeros(near_stats[2].shape, jnp.float32)
    for stats in (near_stats, mid_stats, far_stats):
        factor = jnp.exp(stats[0] - highest)
        denominator = denominator + factor * stats[1]
        numerator = numerator + factor[..., None] * stats[2]
    attended = (numerator / denominator[..., None]).astype(jnp.bfloat16)
    attended = attended.transpose(1, 0, 2, 3).reshape(tok_rows, kv_local * per_group * HEAD_DIM)
    return lax.all_to_all(attended, "tensor", split_axis=0, concat_axis=1, tiled=True)


def solution(mesh):
    in_specs = (
        P(("ctx", "tensor"), None),
        P(("ctx", "tensor"), None),
        P(("ctx", "tensor"), None),
        P("tensor"),
        P("tensor"),
    )
    out_specs = P(("ctx", "tensor"), None)
    return jax.shard_map(
        on_device, mesh=mesh, in_specs=in_specs, out_specs=out_specs, check_vma=False
    )
```

```python
import jax
import jax.numpy as jnp
from jax import lax
from jax.experimental import pallas as pl
from jax.experimental.pallas import tpu as pltpu
from jax.sharding import PartitionSpec as P

HEADS = 32
KV_HEADS = 8
HEAD_DIM = 128
RATE_MID = 8
RATE_FAR = 64


NEG_FILL = -1e30


RING = 8
MESH_IDS = pl.DeviceIdType.MESH


CHUNK = 128


def exchange_body(
    q_ref, kv_ref, mid_ref, fk_ref, fv_ref,
    q_out, prev_out, mid_out, fk_out, fv_out, near_out, max_out, sum_out,
    local_sem, prev_send, prev_recv, q_send, q_recv, x_send, x_recv,
    mid_send, mid_recv, fwd_send, fwd_recv,
    k1_send, k1_recv, v1_send, v1_recv, k2_send, k2_recv, v2_send, v2_recv,
):
    place = lax.axis_index("ctx")
    lane = lax.axis_index("tensor")
    total = 2 * RING * RING
    lanes = q_out.shape[0]
    width = q_out.shape[2]
    kv_local = kv_ref.shape[1] // (2 * HEAD_DIM)
    per_group = width // (kv_local * HEAD_DIM)
    z = lax.rem(place, RING)
    y = lax.rem(place // RING, RING)
    x = place // (RING * RING)

    def at(xi, yi, zi):
        return {"ctx": (xi * RING + yi) * RING + zi}

    def z_peer(step):
        return at(x, y, lax.rem(z + RING + step, RING))

    def y_peer(step):
        return at(x, lax.rem(y + RING + step, RING), z)

    x_peer = at(1 - x, y, z)
    parity = lax.rem(y, 2)
    y_pair = at(x, y + 1 - 2 * parity, z)
    after = {"ctx": lax.rem(place + 1, total)}
    before = {"ctx": lax.rem(place + total - 1, total)}

    barrier = pltpu.get_barrier_semaphore()
    greeted = [x_peer, after, before]
    greeted += [z_peer(step) for step in range(1, RING)]
    greeted += [y_peer(step) for step in range(1, RING)]
    greeted += [{"tensor": lax.rem(lane + step, lanes)} for step in range(1, lanes)]
    for peer in greeted:
        pl.semaphore_signal(barrier, inc=1, device_id=peer, device_id_type=MESH_IDS)
    pl.semaphore_wait(barrier, len(greeted))

    def remote(source, target, send, recv, peer):
        copy = pltpu.make_async_remote_copy(
            src_ref=source, dst_ref=target, send_sem=send, recv_sem=recv,
            device_id=peer, device_id_type=MESH_IDS,
        )
        copy.start()
        return copy

    def columns(index):
        return pl.ds(pl.multiple_of(index * width, width), width)

    class Ring:
        def __init__(self, block, place_in, peer, send, recv, own, hops):
            self.block, self.place, self.peer = block, place_in, peer
            self.send, self.recv, self.own, self.hops = send, recv, own, hops
            self.sent = {}

        def source(self, way, step):
            return lax.rem(self.place + 2 * RING - way * step, RING)

        def start(self, step):
            for slot, way in ((0, 1), (1, -1)):
                if step > self.hops[slot]:
                    continue
                target = self.block(self.source(way, step - 1))
                origin = target
                if step == 1 and self.own is not None:
                    origin = self.own
                index = slot * RING + step
                self.sent[slot, step] = remote(
                    origin, target, self.send.at[index], self.recv.at[index], self.peer(way)
                )

        def landed(self, step):
            found = []
            for slot, way in ((0, 1), (1, -1)):
                if step <= self.hops[slot]:
                    self.sent[slot, step].wait_recv()
                    found.append((slot * RING + step, self.block(self.source(way, step))))
            return found

        def finish(self):
            for copy in self.sent.values():
                copy.wait_send()

    own_k = pltpu.make_async_copy(fk_ref, fk_out.at[y, z, x], local_sem.at[0])
    own_v = pltpu.make_async_copy(fv_ref, fv_out.at[z, y, x], local_sem.at[1])
    own_mid = pltpu.make_async_copy(mid_ref, mid_out.at[parity, z], local_sem.at[2])
    own_q = pltpu.make_async_copy(q_ref.at[:, columns(lane)], q_out.at[lane], local_sem.at[3])
    for copy in (own_k, own_v, own_mid, own_q):
        copy.start()
    x_k = remote(fk_ref, fk_out.at[y, z, x], x_send.at[0], x_recv.at[0], x_peer)
    x_v = remote(fv_ref, fv_out.at[z, y, x], x_send.at[1], x_recv.at[1], x_peer)
    mid_ring = Ring(
        lambda i: mid_out.at[parity, i], z, z_peer, mid_send, mid_recv, mid_ref, (3, 4)
    )
    mid_ring.start(1)
    forwards = [
        remote(mid_ref, mid_out.at[parity, z], fwd_send.at[0], fwd_recv.at[0], y_pair)
    ]
    moves = []
    for step in range(1, lanes):
        other = lax.rem(lane + step, lanes)
        moves.append(
            remote(
                q_ref.at[:, columns(other)], q_out.at[lane],
                q_send.at[step], q_recv.at[step], {"tensor": other},
            )
        )
    chunks = kv_ref.shape[0] // CHUNK
    ahead = {}
    for chunk in reversed(range(chunks)):
        rows = pl.ds(chunk * CHUNK, CHUNK)
        ahead[chunk] = remote(
            kv_ref.at[rows], prev_out.at[rows], prev_send.at[chunk], prev_recv.at[chunk], after
        )
    order = [4, 3, 5, 2, 6, 1, 7]
    own_k.wait()
    own_v.wait()
    x_k.wait_recv()
    x_v.wait_recv()
    firsts_k = {
        step: remote(
            fk_out.at[y, z], fk_out.at[y, z], k1_send.at[step], k1_recv.at[step], z_peer(step)
        )
        for step in order
    }
    firsts_v = {
        step: remote(
            fv_out.at[z, y], fv_out.at[z, y], v1_send.at[step], v1_recv.at[step], y_peer(step)
        )
        for step in order
    }

    def mid_step(step):
        for index, block in mid_ring.landed(step - 1):
            forwards.append(
                remote(block, block, fwd_send.at[index], fwd_recv.at[index], y_pair)
            )
        if step <= 4:
            mid_ring.start(step)

    mid_step(2)
    for step in order:
        firsts_k[step].wait_recv()
        firsts_v[step].wait_recv()
    k_ring = Ring(lambda i: fk_out.at[i], y, y_peer, k2_send, k2_recv, None, (3, 4))
    v_ring = Ring(lambda i: fv_out.at[i], z, z_peer, v2_send, v2_recv, None, (3, 4))
    k_ring.start(1)
    v_ring.start(1)

    def near(chunk):
        first = chunk * CHUNK
        span = kv_ref.shape[0] + CHUNK
        row = lax.broadcasted_iota(jnp.int32, (CHUNK, span), 0)
        col = lax.broadcasted_iota(jnp.int32, (CHUNK, span), 1)
        allowed = (col > row) & (col <= row + kv_ref.shape[0])
        allowed = allowed & ((col >= kv_ref.shape[0] - first) | (place > 0))
        bias = jnp.where(allowed, 0.0, NEG_FILL)
        bias = jnp.concatenate([bias] * per_group, 0)

        @pl.loop(0, kv_local)
        def _(head):
            def window(part):
                cols = pl.ds(
                    pl.multiple_of((part * kv_local + head) * HEAD_DIM, HEAD_DIM), HEAD_DIM
                )
                return jnp.concatenate(
                    [prev_out[first:, cols], kv_ref[: first + CHUNK, cols]], 0
                )

            group = per_group * HEAD_DIM
            wide = q_out[chunk, :, pl.ds(pl.multiple_of(head * group, group), group)]
            rows = jnp.concatenate(
                [wide[:, g * HEAD_DIM : (g + 1) * HEAD_DIM] for g in range(per_group)], 0
            )
            scores = lax.dot_general(
                rows, window(0), (((1,), (1,)), ((), ())), preferred_element_type=jnp.float32
            )
            scores = scores * HEAD_DIM ** (-0.5) + bias
            maxima = jnp.max(scores, axis=1, keepdims=True)
            powers = jnp.exp(scores - maxima)
            totals = jnp.sum(powers, axis=1, keepdims=True)
            weighted = jnp.dot(
                powers.astype(jnp.bfloat16), window(1), preferred_element_type=jnp.float32
            )
            for g in range(per_group):
                mine = slice(g * CHUNK, (g + 1) * CHUNK)
                near_out[head * per_group + g, first : first + CHUNK] = weighted[mine]
                max_out[head * per_group + g, first : first + CHUNK] = maxima[mine]
                sum_out[head * per_group + g, first : first + CHUNK] = totals[mine]

    mid_step(3)
    k_ring.landed(1)
    k_ring.start(2)
    v_ring.landed(1)
    v_ring.start(2)
    own_q.wait()
    ahead[3].wait_recv()
    for copy in moves:
        copy.wait_recv()
    near(3)
    mid_step(4)
    k_ring.landed(2)
    k_ring.start(3)
    v_ring.landed(2)
    v_ring.start(3)
    ahead[2].wait_recv()
    near(2)
    mid_step(5)
    k_ring.landed(3)
    k_ring.start(4)
    v_ring.landed(3)
    v_ring.start(4)
    ahead[1].wait_recv()
    near(1)
    ahead[0].wait_recv()
    near(0)
    k_ring.landed(4)
    v_ring.landed(4)
    for copy in forwards:
        copy.wait_recv()
    own_mid.wait()
    x_k.wait_send()
    x_v.wait_send()
    for step in order:
        firsts_k[step].wait_send()
        firsts_v[step].wait_send()
    for copy in forwards + moves + list(ahead.values()):
        copy.wait_send()
    for ring in (mid_ring, k_ring, v_ring):
        ring.finish()


def exchange(queries, kv_rows, mid_kv, far_k, far_v):
    lanes = lax.axis_size("tensor")
    own, wide = queries.shape
    rows = kv_rows.shape[0]
    heads = HEADS // lanes
    sizes = [4, 4, 4, 4, 4, 2, 2] + [2 * RING] * 12
    stat = jax.ShapeDtypeStruct((heads, rows, 1), jnp.float32)
    return pl.pallas_call(
        exchange_body,
        out_shape=[
            jax.ShapeDtypeStruct((lanes, own, wide // lanes), jnp.bfloat16),
            jax.ShapeDtypeStruct(kv_rows.shape, jnp.bfloat16),
            jax.ShapeDtypeStruct((2, RING) + mid_kv.shape, jnp.bfloat16),
            jax.ShapeDtypeStruct((RING, RING, 2) + far_k.shape, jnp.bfloat16),
            jax.ShapeDtypeStruct((RING, RING, 2) + far_v.shape, jnp.bfloat16),
            jax.ShapeDtypeStruct((heads, rows, HEAD_DIM), jnp.float32),
            stat,
            stat,
        ],
        in_specs=[pl.BlockSpec(memory_space=pltpu.VMEM)] * 5,
        out_specs=[pl.BlockSpec(memory_space=pltpu.VMEM)] * 8,
        scratch_shapes=[pltpu.SemaphoreType.DMA((size,)) for size in sizes],
        compiler_params=pltpu.CompilerParams(
            collective_id=0, has_side_effects=True, vmem_limit_bytes=48 * 2**20
        ),
        name="exchange",
    )(queries, kv_rows, mid_kv, far_k, far_v)


def head_stats(query_rows, key_rows, value_rows, allowed, scale_factor):
    scores = (
        jnp.einsum("agd,bd->agb", query_rows, key_rows, preferred_element_type=jnp.float32)
        * scale_factor
    )
    scores = jnp.where(allowed[:, None, :], scores, NEG_FILL)
    maxima = jnp.max(scores, axis=-1)
    powers = jnp.exp(scores - maxima[..., None])
    totals = jnp.sum(powers, axis=-1)
    weights = powers.astype(jnp.bfloat16)
    weighted = jnp.einsum("agb,bd->agd", weights, value_rows, preferred_element_type=jnp.float32)
    return (maxima, totals, weighted)


def branch_stats(query_rows, kv_rows, allowed, scale_factor):
    query_heads = query_rows.transpose(1, 0, 2, 3)
    key_heads = kv_rows[:, 0].transpose(1, 0, 2)
    value_heads = kv_rows[:, 1].transpose(1, 0, 2)

    def one_head(items):
        return head_stats(items[0], items[1], items[2], allowed, scale_factor)

    return lax.map(one_head, (query_heads, key_heads, value_heads))


def pick_rows(rows, offsets, rate, kv_dim):
    shaped = rows.reshape((rows.shape[0] // rate, rate) + rows.shape[1:])
    chosen = jnp.arange(rate, dtype=jnp.int32)[:, None] == offsets[None, :]
    hit_shape = [1] * shaped.ndim
    hit_shape[1] = rate
    hit_shape[kv_dim + 1] = offsets.shape[0]
    kept = jnp.where(chosen.reshape(hit_shape), shaped, jnp.zeros((), rows.dtype))
    return jnp.sum(kept, axis=1)


def spread_stats(stats, offsets, rate):
    maxima, totals, weighted = stats
    kv_local = maxima.shape[0]
    per_group = maxima.shape[2]
    chosen = jnp.arange(rate, dtype=jnp.int32)[None, :] == offsets[:, None]
    maxima = jnp.where(chosen[:, None, :, None], maxima[:, :, None, :], NEG_FILL).reshape(
        kv_local, -1, per_group
    )
    totals = jnp.where(chosen[:, None, :, None], totals[:, :, None, :], jnp.float32(0.0)).reshape(
        kv_local, -1, per_group
    )
    weighted = jnp.where(chosen[:, None, :, None, None], weighted[:, :, None], jnp.float32(0.0))
    return (maxima, totals, weighted.reshape(kv_local, -1, per_group, weighted.shape[-1]))


def on_device(queries, keys, values, mid_offsets, far_offsets):
    count = lax.axis_size("tensor")
    own = queries.shape[0]
    kv_rows = jnp.concatenate(
        [keys.reshape(own, count, -1), values.reshape(own, count, -1)], axis=2
    ).reshape(own, -1)
    kv_rows = lax.all_to_all(kv_rows, "tensor", split_axis=1, concat_axis=0, tiled=True)
    tok_rows = kv_rows.shape[0]
    kv_local = mid_offsets.shape[0]
    per_group = HEADS // KV_HEADS
    scale_factor = HEAD_DIM ** (-0.5)
    ctx_count = lax.axis_size("ctx")
    ctx_place = lax.axis_index("ctx")
    team_size = min(16, ctx_count)
    kv_dims = (2, kv_local, HEAD_DIM)
    kv_heads = kv_rows.reshape((tok_rows,) + kv_dims)
    mid_kv = pick_rows(kv_heads, mid_offsets, RATE_MID, 2)
    far_kv = pick_rows(kv_heads, far_offsets, RATE_FAR, 2)
    mid_count = tok_rows // RATE_MID
    far_count = tok_rows // RATE_FAR
    far_flat = far_kv.transpose(1, 2, 0, 3).reshape(2, kv_local * far_count, HEAD_DIM)
    gathered, _, mid_all, far_k, far_v, *near = exchange(
        queries, kv_rows, mid_kv.reshape(mid_count, -1), far_flat[0], far_flat[1]
    )
    mid_all = mid_all.reshape((team_size * mid_count,) + kv_dims)
    far_split = (RING, RING, 2, kv_local, far_count, HEAD_DIM)
    far_k = far_k.reshape(far_split).transpose(3, 2, 0, 1, 4, 5)
    far_v = far_v.reshape(far_split).transpose(3, 2, 1, 0, 4, 5)
    far_all = jnp.stack(
        [far_k.reshape(kv_local, -1, HEAD_DIM), far_v.reshape(kv_local, -1, HEAD_DIM)]
    ).transpose(2, 0, 1, 3)
    query_rows = gathered.reshape(tok_rows, kv_local, per_group, HEAD_DIM)
    near = [part.reshape(kv_local, per_group, tok_rows, -1).transpose(0, 2, 1, 3) for part in near]
    near_stats = (near[1][..., 0], near[2][..., 0], near[0])
    mid_queries = pick_rows(query_rows, mid_offsets, RATE_MID, 1)
    far_queries = pick_rows(query_rows, far_offsets, RATE_FAR, 1)
    mid_position = ctx_place % team_size * mid_count + jnp.arange(mid_count)[:, None]
    mid_allowed = jnp.arange(team_size * mid_count)[None, :] <= mid_position
    mid_stats = spread_stats(
        branch_stats(mid_queries, mid_all, mid_allowed, scale_factor), mid_offsets, RATE_MID
    )
    far_position = ctx_place * far_count + jnp.arange(far_count)[:, None]
    far_allowed = jnp.arange(ctx_count * far_count)[None, :] <= far_position
    far_stats = spread_stats(
        branch_stats(far_queries, far_all, far_allowed, scale_factor), far_offsets, RATE_FAR
    )
    highest = jnp.maximum(jnp.maximum(near_stats[0], mid_stats[0]), far_stats[0])
    denominator = jnp.zeros_like(highest)
    numerator = jnp.zeros(near_stats[2].shape, jnp.float32)
    for stats in (near_stats, mid_stats, far_stats):
        factor = jnp.exp(stats[0] - highest)
        denominator = denominator + factor * stats[1]
        numerator = numerator + factor[..., None] * stats[2]
    attended = (numerator / denominator[..., None]).astype(jnp.bfloat16)
    attended = attended.transpose(1, 0, 2, 3).reshape(tok_rows, kv_local * per_group * HEAD_DIM)
    return lax.all_to_all(attended, "tensor", split_axis=0, concat_axis=1, tiled=True)


def solution(mesh):
    in_specs = (
        P(("ctx", "tensor"), None),
        P(("ctx", "tensor"), None),
        P(("ctx", "tensor"), None),
        P("tensor"),
        P("tensor"),
    )
    out_specs = P(("ctx", "tensor"), None)
    return jax.shard_map(
        on_device, mesh=mesh, in_specs=in_specs, out_specs=out_specs, check_vma=False
    )
```

```python
import jax
import jax.numpy as jnp
from jax import lax
from jax.experimental import pallas as pl
from jax.experimental.pallas import tpu as pltpu
from jax.sharding import PartitionSpec as P

HEADS = 32
KV_HEADS = 8
HEAD_DIM = 128
RATE_MID = 8
RATE_FAR = 64


NEG_FILL = -1e30


RING = 8
MESH_IDS = pl.DeviceIdType.MESH


CHUNK = 128


def exchange_body(
    q_ref, kv_ref, mid_ref, fk_ref, fv_ref, mid_off, far_off,
    result,
    q_out, prev_out, mid_out, fk_out, fv_out, near_out, max_out, sum_out, staged,
    local_sem, prev_send, prev_recv, q_send, q_recv, x_send, x_recv,
    mid_send, mid_recv, fwd_send, fwd_recv,
    k1_send, k1_recv, v1_send, v1_recv, k2_send, k2_recv, v2_send, v2_recv,
    back_send, back_recv,
):
    place = lax.axis_index("ctx")
    lane = lax.axis_index("tensor")
    total = 2 * RING * RING
    lanes = q_out.shape[0]
    width = q_out.shape[2]
    kv_local = kv_ref.shape[1] // (2 * HEAD_DIM)
    per_group = width // (kv_local * HEAD_DIM)
    z = lax.rem(place, RING)
    y = lax.rem(place // RING, RING)
    x = place // (RING * RING)

    def at(xi, yi, zi):
        return {"ctx": (xi * RING + yi) * RING + zi}

    def z_peer(step):
        return at(x, y, lax.rem(z + RING + step, RING))

    def y_peer(step):
        return at(x, lax.rem(y + RING + step, RING), z)

    x_peer = at(1 - x, y, z)
    parity = lax.rem(y, 2)
    y_pair = at(x, y + 1 - 2 * parity, z)
    after = {"ctx": lax.rem(place + 1, total)}
    before = {"ctx": lax.rem(place + total - 1, total)}

    barrier = pltpu.get_barrier_semaphore()
    greeted = [x_peer, after, before]
    greeted += [z_peer(step) for step in range(1, RING)]
    greeted += [y_peer(step) for step in range(1, RING)]
    greeted += [{"tensor": lax.rem(lane + step, lanes)} for step in range(1, lanes)]
    for peer in greeted:
        pl.semaphore_signal(barrier, inc=1, device_id=peer, device_id_type=MESH_IDS)
    pl.semaphore_wait(barrier, len(greeted))

    def remote(source, target, send, recv, peer):
        copy = pltpu.make_async_remote_copy(
            src_ref=source, dst_ref=target, send_sem=send, recv_sem=recv,
            device_id=peer, device_id_type=MESH_IDS,
        )
        copy.start()
        return copy

    def columns(index):
        return pl.ds(pl.multiple_of(index * width, width), width)

    class Ring:
        def __init__(self, block, place_in, peer, send, recv, own, hops):
            self.block, self.place, self.peer = block, place_in, peer
            self.send, self.recv, self.own, self.hops = send, recv, own, hops
            self.sent = {}

        def source(self, way, step):
            return lax.rem(self.place + 2 * RING - way * step, RING)

        def start(self, step):
            for slot, way in ((0, 1), (1, -1)):
                if step > self.hops[slot]:
                    continue
                target = self.block(self.source(way, step - 1))
                origin = target
                if step == 1 and self.own is not None:
                    origin = self.own
                index = slot * RING + step
                self.sent[slot, step] = remote(
                    origin, target, self.send.at[index], self.recv.at[index], self.peer(way)
                )

        def landed(self, step):
            found = []
            for slot, way in ((0, 1), (1, -1)):
                if step <= self.hops[slot]:
                    self.sent[slot, step].wait_recv()
                    found.append((slot * RING + step, self.block(self.source(way, step))))
            return found

        def finish(self):
            for copy in self.sent.values():
                copy.wait_send()

    own_k = pltpu.make_async_copy(fk_ref, fk_out.at[y, z, x], local_sem.at[0])
    own_v = pltpu.make_async_copy(fv_ref, fv_out.at[z, y, x], local_sem.at[1])
    own_mid = pltpu.make_async_copy(mid_ref, mid_out.at[parity, z], local_sem.at[2])
    own_q = pltpu.make_async_copy(q_ref.at[:, columns(lane)], q_out.at[lane], local_sem.at[3])
    for copy in (own_k, own_v, own_mid, own_q):
        copy.start()
    x_k = remote(fk_ref, fk_out.at[y, z, x], x_send.at[0], x_recv.at[0], x_peer)
    x_v = remote(fv_ref, fv_out.at[z, y, x], x_send.at[1], x_recv.at[1], x_peer)
    mid_ring = Ring(
        lambda i: mid_out.at[parity, i], z, z_peer, mid_send, mid_recv, mid_ref, (3, 4)
    )
    mid_ring.start(1)
    forwards = [
        remote(mid_ref, mid_out.at[parity, z], fwd_send.at[0], fwd_recv.at[0], y_pair)
    ]
    moves = []
    for step in range(1, lanes):
        other = lax.rem(lane + step, lanes)
        moves.append(
            remote(
                q_ref.at[:, columns(other)], q_out.at[lane],
                q_send.at[step], q_recv.at[step], {"tensor": other},
            )
        )
    chunks = kv_ref.shape[0] // CHUNK
    ahead = {}
    for chunk in reversed(range(chunks)):
        rows = pl.ds(chunk * CHUNK, CHUNK)
        ahead[chunk] = remote(
            kv_ref.at[rows], prev_out.at[rows], prev_send.at[chunk], prev_recv.at[chunk], after
        )
    order = [4, 3, 5, 2, 6, 1, 7]
    own_k.wait()
    own_v.wait()
    x_k.wait_recv()
    x_v.wait_recv()
    firsts_k = {
        step: remote(
            fk_out.at[y, z], fk_out.at[y, z], k1_send.at[step], k1_recv.at[step], z_peer(step)
        )
        for step in order
    }
    firsts_v = {
        step: remote(
            fv_out.at[z, y], fv_out.at[z, y], v1_send.at[step], v1_recv.at[step], y_peer(step)
        )
        for step in order
    }

    def mid_step(step):
        for index, block in mid_ring.landed(step - 1):
            forwards.append(
                remote(block, block, fwd_send.at[index], fwd_recv.at[index], y_pair)
            )
        if step <= 4:
            mid_ring.start(step)

    mid_step(2)
    for step in order:
        firsts_k[step].wait_recv()
        firsts_v[step].wait_recv()
    k_ring = Ring(lambda i: fk_out.at[i], y, y_peer, k2_send, k2_recv, None, (3, 4))
    v_ring = Ring(lambda i: fv_out.at[i], z, z_peer, v2_send, v2_recv, None, (3, 4))
    k_ring.start(1)
    v_ring.start(1)

    def near(chunk):
        first = chunk * CHUNK
        span = kv_ref.shape[0] + CHUNK
        row = lax.broadcasted_iota(jnp.int32, (CHUNK, span), 0)
        col = lax.broadcasted_iota(jnp.int32, (CHUNK, span), 1)
        allowed = (col > row) & (col <= row + kv_ref.shape[0])
        allowed = allowed & ((col >= kv_ref.shape[0] - first) | (place > 0))
        bias = jnp.where(allowed, 0.0, NEG_FILL)
        bias = jnp.concatenate([bias] * per_group, 0)

        @pl.loop(0, kv_local)
        def _(head):
            def window(part):
                cols = pl.ds(
                    pl.multiple_of((part * kv_local + head) * HEAD_DIM, HEAD_DIM), HEAD_DIM
                )
                return jnp.concatenate(
                    [prev_out[first:, cols], kv_ref[: first + CHUNK, cols]], 0
                )

            group = per_group * HEAD_DIM
            wide = q_out[chunk, :, pl.ds(pl.multiple_of(head * group, group), group)]
            rows = jnp.concatenate(
                [wide[:, g * HEAD_DIM : (g + 1) * HEAD_DIM] for g in range(per_group)], 0
            )
            scores = lax.dot_general(
                rows, window(0), (((1,), (1,)), ((), ())), preferred_element_type=jnp.float32
            )
            scores = scores * HEAD_DIM ** (-0.5) + bias
            maxima = jnp.max(scores, axis=1, keepdims=True)
            powers = jnp.exp(scores - maxima)
            totals = jnp.sum(powers, axis=1, keepdims=True)
            weighted = jnp.dot(
                powers.astype(jnp.bfloat16), window(1), preferred_element_type=jnp.float32
            )
            for g in range(per_group):
                mine = slice(g * CHUNK, (g + 1) * CHUNK)
                near_out[head * per_group + g, first : first + CHUNK] = weighted[mine]
                max_out[head * per_group + g, first : first + CHUNK] = maxima[mine]
                sum_out[head * per_group + g, first : first + CHUNK] = totals[mine]

    mid_step(3)
    k_ring.landed(1)
    k_ring.start(2)
    v_ring.landed(1)
    v_ring.start(2)
    own_q.wait()
    ahead[3].wait_recv()
    for copy in moves:
        copy.wait_recv()
    near(3)
    mid_step(4)
    k_ring.landed(2)
    k_ring.start(3)
    v_ring.landed(2)
    v_ring.start(3)
    ahead[2].wait_recv()
    near(2)
    mid_step(5)
    k_ring.landed(3)
    k_ring.start(4)
    v_ring.landed(3)
    v_ring.start(4)
    ahead[1].wait_recv()
    near(1)
    ahead[0].wait_recv()
    near(0)
    own_mid.wait()
    for copy in forwards:
        copy.wait_recv()
    tokens = kv_ref.shape[0]
    group = per_group * HEAD_DIM

    def picked(head, offset, rate):
        count = tokens // rate
        row = lax.broadcasted_iota(jnp.int32, (count, tokens), 0)
        col = lax.broadcasted_iota(jnp.int32, (count, tokens), 1)
        chosen = jnp.where(col == row * rate + offset, 1.0, 0.0).astype(jnp.bfloat16)
        wide = q_out[:, :, head * group : (head + 1) * group].reshape(tokens, group)
        rows = jnp.dot(chosen, wide, preferred_element_type=jnp.float32)
        parts = [rows[:, g * HEAD_DIM : (g + 1) * HEAD_DIM] for g in range(per_group)]
        return jnp.concatenate(parts, 0).astype(jnp.bfloat16)

    def attend(rows, key_rows, value_rows, bias):
        scores = lax.dot_general(
            rows, key_rows, (((1,), (1,)), ((), ())), preferred_element_type=jnp.float32
        )
        scores = scores * HEAD_DIM ** (-0.5) + jnp.concatenate([bias] * per_group, 0)
        maxima = jnp.max(scores, axis=1, keepdims=True)
        powers = jnp.exp(scores - maxima)
        totals = jnp.sum(powers, axis=1, keepdims=True)
        weighted = jnp.dot(
            powers.astype(jnp.bfloat16), value_rows, preferred_element_type=jnp.float32
        )
        return maxima, totals, weighted

    def mid_stats(head):
        count = tokens // RATE_MID
        span = 2 * RING * count
        row = lax.broadcasted_iota(jnp.int32, (count, span), 0)
        col = lax.broadcasted_iota(jnp.int32, (count, span), 1)
        bias = jnp.where(col <= lax.rem(place, 2 * RING) * count + row, 0.0, NEG_FILL)
        first = head * HEAD_DIM
        second = (kv_local + head) * HEAD_DIM
        return attend(
            picked(head, mid_off[head], RATE_MID),
            mid_out[:, :, :, first : first + HEAD_DIM].reshape(span, HEAD_DIM),
            mid_out[:, :, :, second : second + HEAD_DIM].reshape(span, HEAD_DIM),
            bias,
        )

    mids = [mid_stats(head) for head in range(kv_local)]
    k_ring.landed(4)
    v_ring.landed(4)

    def far_stats(head):
        count = tokens // RATE_FAR
        span = total * kv_local * count
        row = lax.broadcasted_iota(jnp.int32, (count, span), 0)
        col = lax.broadcasted_iota(jnp.int32, (count, span), 1)
        inner = lax.rem(col, count)
        owner = lax.rem(col // count, kv_local)
        block = col // (count * kv_local)
        source = lax.rem(block, 2) * (RING * RING) + block // 2
        allowed = (owner == head) & (source * count + inner <= place * count + row)
        key_rows = fk_out[...].reshape(span, HEAD_DIM)
        value_rows = jnp.concatenate(
            [fv_out[:, i].reshape(span // RING, HEAD_DIM) for i in range(RING)], 0
        )
        return attend(
            picked(head, far_off[head], RATE_FAR),
            key_rows, value_rows, jnp.where(allowed, 0.0, NEG_FILL),
        )

    fars = [far_stats(head) for head in range(kv_local)]
    token = lax.broadcasted_iota(jnp.int32, (tokens, HEAD_DIM), 0)

    def spread(stats, head, g, offset, rate):
        count = tokens // rate
        full = []
        for part in stats:
            part = jnp.broadcast_to(part[g * count : (g + 1) * count], (count, HEAD_DIM))
            part = jnp.broadcast_to(part[:, None, :], (count, rate, HEAD_DIM))
            full.append(part.reshape(tokens, HEAD_DIM))
        full[0] = jnp.where(lax.rem(token, rate) == offset, full[0], NEG_FILL)
        return full

    def send_back(head):
        for step in range(1, lanes):
            other = lax.rem(lane + step, lanes)
            start = pl.multiple_of(lane * width + head * group, group)
            backs.append(
                remote(
                    staged.at[other, :, pl.ds(head * group, group)],
                    result.at[:, pl.ds(start, group)],
                    back_send.at[head, step], back_recv.at[head, step], {"tensor": other},
                )
            )

    backs = []
    for head in range(kv_local):
        for g in range(per_group):
            index = head * per_group + g
            near_parts = (
                jnp.broadcast_to(max_out[index], (tokens, HEAD_DIM)),
                jnp.broadcast_to(sum_out[index], (tokens, HEAD_DIM)),
                near_out[index],
            )
            branches = (
                near_parts,
                spread(mids[head], head, g, mid_off[head], RATE_MID),
                spread(fars[head], head, g, far_off[head], RATE_FAR),
            )
            highest = jnp.maximum(
                jnp.maximum(branches[0][0], branches[1][0]), branches[2][0]
            )
            numerator = jnp.zeros((tokens, HEAD_DIM), jnp.float32)
            denominator = jnp.zeros((tokens, HEAD_DIM), jnp.float32)
            for maxima, totals, weighted in branches:
                factor = jnp.exp(maxima - highest)
                denominator = denominator + factor * totals
                numerator = numerator + factor * weighted
            attended = (numerator / denominator).astype(jnp.bfloat16)
            staged[:, :, index * HEAD_DIM : (index + 1) * HEAD_DIM] = attended.reshape(
                lanes, tokens // lanes, HEAD_DIM
            )
            if head > 0 and g == 0:
                send_back(head - 1)
    send_back(kv_local - 1)
    own_back = pltpu.make_async_copy(
        staged.at[lane], result.at[:, columns(lane)], local_sem.at[4]
    )
    own_back.start()
    x_k.wait_send()
    x_v.wait_send()
    for step in order:
        firsts_k[step].wait_send()
        firsts_v[step].wait_send()
    for copy in forwards + moves + list(ahead.values()):
        copy.wait_send()
    for ring in (mid_ring, k_ring, v_ring):
        ring.finish()
    own_back.wait()
    for copy in backs:
        copy.wait()


def exchange(queries, kv_rows, mid_kv, far_k, far_v, mid_offsets, far_offsets):
    lanes = lax.axis_size("tensor")
    own, wide = queries.shape
    rows = kv_rows.shape[0]
    heads = HEADS // lanes
    kv_local = mid_offsets.shape[0]
    sizes = [5, 4, 4, 4, 4, 2, 2] + [2 * RING] * 12
    vmem = pl.BlockSpec(memory_space=pltpu.VMEM)
    smem = pl.BlockSpec(memory_space=pltpu.SMEM)
    return pl.pallas_call(
        exchange_body,
        out_shape=jax.ShapeDtypeStruct((own, wide), jnp.bfloat16),
        in_specs=[vmem] * 5 + [smem] * 2,
        out_specs=vmem,
        scratch_shapes=[
            pltpu.VMEM((lanes, own, wide // lanes), jnp.bfloat16),
            pltpu.VMEM(kv_rows.shape, jnp.bfloat16),
            pltpu.VMEM((2, RING) + mid_kv.shape, jnp.bfloat16),
            pltpu.VMEM((RING, RING, 2) + far_k.shape, jnp.bfloat16),
            pltpu.VMEM((RING, RING, 2) + far_v.shape, jnp.bfloat16),
            pltpu.VMEM((heads, rows, HEAD_DIM), jnp.float32),
            pltpu.VMEM((heads, rows, 1), jnp.float32),
            pltpu.VMEM((heads, rows, 1), jnp.float32),
            pltpu.VMEM((lanes, own, wide // lanes), jnp.bfloat16),
        ]
        + [pltpu.SemaphoreType.DMA((size,)) for size in sizes]
        + [pltpu.SemaphoreType.DMA((kv_local, lanes))] * 2,
        compiler_params=pltpu.CompilerParams(
            collective_id=0, has_side_effects=True, vmem_limit_bytes=56 * 2**20
        ),
        name="exchange",
    )(queries, kv_rows, mid_kv, far_k, far_v, mid_offsets, far_offsets)


def pick_rows(rows, offsets, rate, kv_dim):
    shaped = rows.reshape((rows.shape[0] // rate, rate) + rows.shape[1:])
    chosen = jnp.arange(rate, dtype=jnp.int32)[:, None] == offsets[None, :]
    hit_shape = [1] * shaped.ndim
    hit_shape[1] = rate
    hit_shape[kv_dim + 1] = offsets.shape[0]
    kept = jnp.where(chosen.reshape(hit_shape), shaped, jnp.zeros((), rows.dtype))
    return jnp.sum(kept, axis=1)


def on_device(queries, keys, values, mid_offsets, far_offsets):
    count = lax.axis_size("tensor")
    own = queries.shape[0]
    kv_rows = jnp.concatenate(
        [keys.reshape(own, count, -1), values.reshape(own, count, -1)], axis=2
    ).reshape(own, -1)
    kv_rows = lax.all_to_all(kv_rows, "tensor", split_axis=1, concat_axis=0, tiled=True)
    tok_rows = kv_rows.shape[0]
    kv_local = mid_offsets.shape[0]
    kv_dims = (2, kv_local, HEAD_DIM)
    kv_heads = kv_rows.reshape((tok_rows,) + kv_dims)
    mid_kv = pick_rows(kv_heads, mid_offsets, RATE_MID, 2)
    far_kv = pick_rows(kv_heads, far_offsets, RATE_FAR, 2)
    mid_count = tok_rows // RATE_MID
    far_count = tok_rows // RATE_FAR
    far_flat = far_kv.transpose(1, 2, 0, 3).reshape(2, kv_local * far_count, HEAD_DIM)
    return exchange(
        queries, kv_rows, mid_kv.reshape(mid_count, -1), far_flat[0], far_flat[1],
        mid_offsets, far_offsets,
    )


def solution(mesh):
    in_specs = (
        P(("ctx", "tensor"), None),
        P(("ctx", "tensor"), None),
        P(("ctx", "tensor"), None),
        P("tensor"),
        P("tensor"),
    )
    out_specs = P(("ctx", "tensor"), None)
    return jax.shard_map(
        on_device, mesh=mesh, in_specs=in_specs, out_specs=out_specs, check_vma=False
    )
```

```python
import jax
import jax.numpy as jnp
from jax import lax
from jax.experimental import pallas as pl
from jax.experimental.pallas import tpu as pltpu
from jax.sharding import PartitionSpec as P

HEADS = 32
KV_HEADS = 8
HEAD_DIM = 128
RATE_MID = 8
RATE_FAR = 64


NEG_FILL = -1e30


RING = 8
MESH_IDS = pl.DeviceIdType.MESH


CHUNK = 128


def exchange_body(
    q_ref, key_ref, value_ref, mid_off, far_off,
    result,
    kv_ref, mid_ref, fk_ref, fv_ref,
    q_out, prev_out, mid_out, fk_out, fv_out, near_out, max_out, sum_out, staged,
    local_sem, prev_send, prev_recv, q_send, q_recv, x_send, x_recv,
    mid_send, mid_recv, fwd_send, fwd_recv,
    k1_send, k1_recv, v1_send, v1_recv, k2_send, k2_recv, v2_send, v2_recv,
    back_send, back_recv, kv_send, kv_recv,
):
    place = lax.axis_index("ctx")
    lane = lax.axis_index("tensor")
    total = 2 * RING * RING
    lanes = q_out.shape[0]
    width = q_out.shape[2]
    kv_local = kv_ref.shape[1] // (2 * HEAD_DIM)
    per_group = width // (kv_local * HEAD_DIM)
    z = lax.rem(place, RING)
    y = lax.rem(place // RING, RING)
    x = place // (RING * RING)

    def at(xi, yi, zi):
        return {"ctx": (xi * RING + yi) * RING + zi}

    def z_peer(step):
        return at(x, y, lax.rem(z + RING + step, RING))

    def y_peer(step):
        return at(x, lax.rem(y + RING + step, RING), z)

    x_peer = at(1 - x, y, z)
    parity = lax.rem(y, 2)
    y_pair = at(x, y + 1 - 2 * parity, z)
    after = {"ctx": lax.rem(place + 1, total)}
    before = {"ctx": lax.rem(place + total - 1, total)}

    barrier = pltpu.get_barrier_semaphore()
    greeted = [x_peer, after, before]
    greeted += [z_peer(step) for step in range(1, RING)]
    greeted += [y_peer(step) for step in range(1, RING)]
    greeted += [{"tensor": lax.rem(lane + step, lanes)} for step in range(1, lanes)]
    for peer in greeted:
        pl.semaphore_signal(barrier, inc=1, device_id=peer, device_id_type=MESH_IDS)
    pl.semaphore_wait(barrier, len(greeted))

    def remote(source, target, send, recv, peer):
        copy = pltpu.make_async_remote_copy(
            src_ref=source, dst_ref=target, send_sem=send, recv_sem=recv,
            device_id=peer, device_id_type=MESH_IDS,
        )
        copy.start()
        return copy

    def columns(index):
        return pl.ds(pl.multiple_of(index * width, width), width)

    class Ring:
        def __init__(self, block, place_in, peer, send, recv, own, hops):
            self.block, self.place, self.peer = block, place_in, peer
            self.send, self.recv, self.own, self.hops = send, recv, own, hops
            self.sent = {}

        def source(self, way, step):
            return lax.rem(self.place + 2 * RING - way * step, RING)

        def start(self, step):
            for slot, way in ((0, 1), (1, -1)):
                if step > self.hops[slot]:
                    continue
                target = self.block(self.source(way, step - 1))
                origin = target
                if step == 1 and self.own is not None:
                    origin = self.own
                index = slot * RING + step
                self.sent[slot, step] = remote(
                    origin, target, self.send.at[index], self.recv.at[index], self.peer(way)
                )

        def landed(self, step):
            found = []
            for slot, way in ((0, 1), (1, -1)):
                if step <= self.hops[slot]:
                    self.sent[slot, step].wait_recv()
                    found.append((slot * RING + step, self.block(self.source(way, step))))
            return found

        def finish(self):
            for copy in self.sent.values():
                copy.wait_send()

    tokens, kv_wide = kv_ref.shape
    half = kv_wide // 2
    mine_rows = pl.ds(pl.multiple_of(lane * CHUNK, CHUNK), CHUNK)

    def kv_columns(index):
        return pl.ds(pl.multiple_of(index * half, half), half)

    shares = []
    for part, source in enumerate((key_ref, value_ref)):
        target = kv_ref.at[mine_rows, pl.ds(part * half, half)]
        own_part = pltpu.make_async_copy(
            source.at[:, kv_columns(lane)], target, local_sem.at[5 + part]
        )
        own_part.start()
        shares.append((own_part, target))
    arriving = []
    for step in (2, 1, 3):
        other = lax.rem(lane + step, lanes)
        for part, source in enumerate((key_ref, value_ref)):
            arriving.append(
                remote(
                    source.at[:, kv_columns(other)], shares[part][1],
                    kv_send.at[part, step], kv_recv.at[part, step], {"tensor": other},
                )
            )
    own_q = pltpu.make_async_copy(q_ref.at[:, columns(lane)], q_out.at[lane], local_sem.at[3])
    own_q.start()
    moves = []
    for step in range(1, lanes):
        other = lax.rem(lane + step, lanes)
        moves.append(
            remote(
                q_ref.at[:, columns(other)], q_out.at[lane],
                q_send.at[step], q_recv.at[step], {"tensor": other},
            )
        )
    for own_part, _ in shares:
        own_part.wait()
    for copy in arriving:
        copy.wait_recv()

    def one_hot(offset, rate):
        count = tokens // rate
        row = lax.broadcasted_iota(jnp.int32, (count, tokens), 0)
        col = lax.broadcasted_iota(jnp.int32, (count, tokens), 1)
        return jnp.where(col == row * rate + offset, 1.0, 0.0).astype(jnp.bfloat16)

    mid_hot = [one_hot(mid_off[head], RATE_MID) for head in range(kv_local)]
    far_hot = [one_hot(far_off[head], RATE_FAR) for head in range(kv_local)]
    far_rows = []
    for part in range(2):
        for head in range(kv_local):
            cols = slice((part * kv_local + head) * HEAD_DIM, (part * kv_local + head + 1) * HEAD_DIM)
            block = kv_ref[:, cols]
            mid_ref[:, cols] = jnp.dot(
                mid_hot[head], block, preferred_element_type=jnp.float32
            ).astype(jnp.bfloat16)
            far_rows.append(
                jnp.dot(far_hot[head], block, preferred_element_type=jnp.float32)
            )
    fk_ref[...] = jnp.concatenate(far_rows[:kv_local], 0).astype(jnp.bfloat16)
    fv_ref[...] = jnp.concatenate(far_rows[kv_local:], 0).astype(jnp.bfloat16)

    own_mid = pltpu.make_async_copy(mid_ref, mid_out.at[parity, z], local_sem.at[2])
    own_mid.start()
    mid_ring = Ring(
        lambda i: mid_out.at[parity, i], z, z_peer, mid_send, mid_recv, mid_ref, (3, 4)
    )
    mid_ring.start(1)
    forwards = [
        remote(mid_ref, mid_out.at[parity, z], fwd_send.at[0], fwd_recv.at[0], y_pair)
    ]
    own_k = pltpu.make_async_copy(fk_ref, fk_out.at[y, z, x], local_sem.at[0])
    own_v = pltpu.make_async_copy(fv_ref, fv_out.at[z, y, x], local_sem.at[1])
    own_k.start()
    own_v.start()
    x_k = remote(fk_ref, fk_out.at[y, z, x], x_send.at[0], x_recv.at[0], x_peer)
    x_v = remote(fv_ref, fv_out.at[z, y, x], x_send.at[1], x_recv.at[1], x_peer)
    ahead = {}

    def pass_on(chunk):
        rows = pl.ds(chunk * CHUNK, CHUNK)
        ahead[chunk] = remote(
            kv_ref.at[rows], prev_out.at[rows], prev_send.at[chunk], prev_recv.at[chunk], after
        )

    order = [4, 3, 5, 2, 6, 1, 7]
    pass_on(3)
    own_k.wait()
    own_v.wait()
    x_k.wait_recv()
    x_v.wait_recv()
    firsts_k = {
        step: remote(
            fk_out.at[y, z], fk_out.at[y, z], k1_send.at[step], k1_recv.at[step], z_peer(step)
        )
        for step in order
    }
    firsts_v = {
        step: remote(
            fv_out.at[z, y], fv_out.at[z, y], v1_send.at[step], v1_recv.at[step], y_peer(step)
        )
        for step in order
    }

    def mid_step(step):
        for index, block in mid_ring.landed(step - 1):
            forwards.append(
                remote(block, block, fwd_send.at[index], fwd_recv.at[index], y_pair)
            )
        if step <= 4:
            mid_ring.start(step)

    mid_step(2)
    pass_on(2)
    for step in order:
        firsts_k[step].wait_recv()
        firsts_v[step].wait_recv()
    k_ring = Ring(lambda i: fk_out.at[i], y, y_peer, k2_send, k2_recv, None, (3, 4))
    v_ring = Ring(lambda i: fv_out.at[i], z, z_peer, v2_send, v2_recv, None, (3, 4))
    k_ring.start(1)
    v_ring.start(1)

    def near(chunk):
        first = chunk * CHUNK
        span = kv_ref.shape[0] + CHUNK
        row = lax.broadcasted_iota(jnp.int32, (CHUNK, span), 0)
        col = lax.broadcasted_iota(jnp.int32, (CHUNK, span), 1)
        allowed = (col > row) & (col <= row + kv_ref.shape[0])
        allowed = allowed & ((col >= kv_ref.shape[0] - first) | (place > 0))
        bias = jnp.where(allowed, 0.0, NEG_FILL)
        bias = jnp.concatenate([bias] * per_group, 0)

        @pl.loop(0, kv_local)
        def _(head):
            def window(part):
                cols = pl.ds(
                    pl.multiple_of((part * kv_local + head) * HEAD_DIM, HEAD_DIM), HEAD_DIM
                )
                return jnp.concatenate(
                    [prev_out[first:, cols], kv_ref[: first + CHUNK, cols]], 0
                )

            group = per_group * HEAD_DIM
            wide = q_out[chunk, :, pl.ds(pl.multiple_of(head * group, group), group)]
            rows = jnp.concatenate(
                [wide[:, g * HEAD_DIM : (g + 1) * HEAD_DIM] for g in range(per_group)], 0
            )
            scores = lax.dot_general(
                rows, window(0), (((1,), (1,)), ((), ())), preferred_element_type=jnp.float32
            )
            scores = scores * HEAD_DIM ** (-0.5) + bias
            maxima = jnp.max(scores, axis=1, keepdims=True)
            powers = jnp.exp(scores - maxima)
            totals = jnp.sum(powers, axis=1, keepdims=True)
            weighted = jnp.dot(
                powers.astype(jnp.bfloat16), window(1), preferred_element_type=jnp.float32
            )
            for g in range(per_group):
                mine = slice(g * CHUNK, (g + 1) * CHUNK)
                near_out[head * per_group + g, first : first + CHUNK] = weighted[mine]
                max_out[head * per_group + g, first : first + CHUNK] = maxima[mine]
                sum_out[head * per_group + g, first : first + CHUNK] = totals[mine]

    mid_step(3)
    pass_on(1)
    own_q.wait()
    for copy in moves:
        copy.wait_recv()
    k_ring.landed(1)
    k_ring.start(2)
    v_ring.landed(1)
    v_ring.start(2)
    pass_on(0)
    ahead[3].wait_recv()
    near(3)
    mid_step(4)
    k_ring.landed(2)
    k_ring.start(3)
    v_ring.landed(2)
    v_ring.start(3)
    ahead[2].wait_recv()
    near(2)
    mid_step(5)
    k_ring.landed(3)
    k_ring.start(4)
    v_ring.landed(3)
    v_ring.start(4)
    ahead[1].wait_recv()
    near(1)
    ahead[0].wait_recv()
    near(0)
    own_mid.wait()
    for copy in forwards:
        copy.wait_recv()
    group = per_group * HEAD_DIM

    def picked(head, chosen):
        wide = q_out[:, :, head * group : (head + 1) * group].reshape(tokens, group)
        rows = jnp.dot(chosen, wide, preferred_element_type=jnp.float32)
        parts = [rows[:, g * HEAD_DIM : (g + 1) * HEAD_DIM] for g in range(per_group)]
        return jnp.concatenate(parts, 0).astype(jnp.bfloat16)

    def attend(rows, key_rows, value_rows, bias):
        scores = lax.dot_general(
            rows, key_rows, (((1,), (1,)), ((), ())), preferred_element_type=jnp.float32
        )
        scores = scores * HEAD_DIM ** (-0.5) + jnp.concatenate([bias] * per_group, 0)
        maxima = jnp.max(scores, axis=1, keepdims=True)
        powers = jnp.exp(scores - maxima)
        totals = jnp.sum(powers, axis=1, keepdims=True)
        weighted = jnp.dot(
            powers.astype(jnp.bfloat16), value_rows, preferred_element_type=jnp.float32
        )
        return maxima, totals, weighted

    def mid_stats(head):
        count = tokens // RATE_MID
        span = 2 * RING * count
        row = lax.broadcasted_iota(jnp.int32, (count, span), 0)
        col = lax.broadcasted_iota(jnp.int32, (count, span), 1)
        bias = jnp.where(col <= lax.rem(place, 2 * RING) * count + row, 0.0, NEG_FILL)
        first = head * HEAD_DIM
        second = (kv_local + head) * HEAD_DIM
        return attend(
            picked(head, mid_hot[head]),
            mid_out[:, :, :, first : first + HEAD_DIM].reshape(span, HEAD_DIM),
            mid_out[:, :, :, second : second + HEAD_DIM].reshape(span, HEAD_DIM),
            bias,
        )

    mids = [mid_stats(head) for head in range(kv_local)]
    k_ring.landed(4)
    v_ring.landed(4)

    def far_stats(head):
        count = tokens // RATE_FAR
        span = total * kv_local * count
        row = lax.broadcasted_iota(jnp.int32, (count, span), 0)
        col = lax.broadcasted_iota(jnp.int32, (count, span), 1)
        inner = lax.rem(col, count)
        owner = lax.rem(col // count, kv_local)
        block = col // (count * kv_local)
        source = lax.rem(block, 2) * (RING * RING) + block // 2
        allowed = (owner == head) & (source * count + inner <= place * count + row)
        key_rows = fk_out[...].reshape(span, HEAD_DIM)
        value_rows = jnp.concatenate(
            [fv_out[:, i].reshape(span // RING, HEAD_DIM) for i in range(RING)], 0
        )
        return attend(
            picked(head, far_hot[head]),
            key_rows, value_rows, jnp.where(allowed, 0.0, NEG_FILL),
        )

    fars = [far_stats(head) for head in range(kv_local)]
    token = lax.broadcasted_iota(jnp.int32, (tokens, HEAD_DIM), 0)

    def spread(stats, head, g, offset, rate):
        count = tokens // rate
        full = []
        for part in stats:
            part = jnp.broadcast_to(part[g * count : (g + 1) * count], (count, HEAD_DIM))
            part = jnp.broadcast_to(part[:, None, :], (count, rate, HEAD_DIM))
            full.append(part.reshape(tokens, HEAD_DIM))
        full[0] = jnp.where(lax.rem(token, rate) == offset, full[0], NEG_FILL)
        return full

    def send_back(head):
        for step in range(1, lanes):
            other = lax.rem(lane + step, lanes)
            start = pl.multiple_of(lane * width + head * group, group)
            backs.append(
                remote(
                    staged.at[other, :, pl.ds(head * group, group)],
                    result.at[:, pl.ds(start, group)],
                    back_send.at[head, step], back_recv.at[head, step], {"tensor": other},
                )
            )

    backs = []
    for head in range(kv_local):
        for g in range(per_group):
            index = head * per_group + g
            near_parts = (
                jnp.broadcast_to(max_out[index], (tokens, HEAD_DIM)),
                jnp.broadcast_to(sum_out[index], (tokens, HEAD_DIM)),
                near_out[index],
            )
            branches = (
                near_parts,
                spread(mids[head], head, g, mid_off[head], RATE_MID),
                spread(fars[head], head, g, far_off[head], RATE_FAR),
            )
            highest = jnp.maximum(
                jnp.maximum(branches[0][0], branches[1][0]), branches[2][0]
            )
            numerator = jnp.zeros((tokens, HEAD_DIM), jnp.float32)
            denominator = jnp.zeros((tokens, HEAD_DIM), jnp.float32)
            for maxima, totals, weighted in branches:
                factor = jnp.exp(maxima - highest)
                denominator = denominator + factor * totals
                numerator = numerator + factor * weighted
            attended = (numerator / denominator).astype(jnp.bfloat16)
            staged[:, :, index * HEAD_DIM : (index + 1) * HEAD_DIM] = attended.reshape(
                lanes, tokens // lanes, HEAD_DIM
            )
            if head > 0 and g == 0:
                send_back(head - 1)
    send_back(kv_local - 1)
    own_back = pltpu.make_async_copy(
        staged.at[lane], result.at[:, columns(lane)], local_sem.at[4]
    )
    own_back.start()
    x_k.wait_send()
    x_v.wait_send()
    for step in order:
        firsts_k[step].wait_send()
        firsts_v[step].wait_send()
    for copy in arriving + forwards + moves + list(ahead.values()):
        copy.wait_send()
    for ring in (mid_ring, k_ring, v_ring):
        ring.finish()
    own_back.wait()
    for copy in backs:
        copy.wait()


def exchange(queries, keys, values, mid_offsets, far_offsets):
    lanes = lax.axis_size("tensor")
    own, wide = queries.shape
    rows = own * lanes
    heads = HEADS // lanes
    kv_local = mid_offsets.shape[0]
    kv_shape = (rows, 2 * kv_local * HEAD_DIM)
    mid_shape = (rows // RATE_MID, kv_shape[1])
    far_shape = (kv_local * rows // RATE_FAR, HEAD_DIM)
    sizes = [7, 4, 4, 4, 4, 2, 2] + [2 * RING] * 12
    vmem = pl.BlockSpec(memory_space=pltpu.VMEM)
    smem = pl.BlockSpec(memory_space=pltpu.SMEM)
    return pl.pallas_call(
        exchange_body,
        out_shape=jax.ShapeDtypeStruct((own, wide), jnp.bfloat16),
        in_specs=[vmem] * 3 + [smem] * 2,
        out_specs=vmem,
        scratch_shapes=[
            pltpu.VMEM(kv_shape, jnp.bfloat16),
            pltpu.VMEM(mid_shape, jnp.bfloat16),
            pltpu.VMEM(far_shape, jnp.bfloat16),
            pltpu.VMEM(far_shape, jnp.bfloat16),
            pltpu.VMEM((lanes, own, wide // lanes), jnp.bfloat16),
            pltpu.VMEM(kv_shape, jnp.bfloat16),
            pltpu.VMEM((2, RING) + mid_shape, jnp.bfloat16),
            pltpu.VMEM((RING, RING, 2) + far_shape, jnp.bfloat16),
            pltpu.VMEM((RING, RING, 2) + far_shape, jnp.bfloat16),
            pltpu.VMEM((heads, rows, HEAD_DIM), jnp.float32),
            pltpu.VMEM((heads, rows, 1), jnp.float32),
            pltpu.VMEM((heads, rows, 1), jnp.float32),
            pltpu.VMEM((lanes, own, wide // lanes), jnp.bfloat16),
        ]
        + [pltpu.SemaphoreType.DMA((size,)) for size in sizes]
        + [pltpu.SemaphoreType.DMA((kv_local, lanes))] * 2
        + [pltpu.SemaphoreType.DMA((2, lanes))] * 2,
        compiler_params=pltpu.CompilerParams(
            collective_id=0, has_side_effects=True, vmem_limit_bytes=56 * 2**20
        ),
        name="exchange",
    )(queries, keys, values, mid_offsets, far_offsets)


def solution(mesh):
    in_specs = (
        P(("ctx", "tensor"), None),
        P(("ctx", "tensor"), None),
        P(("ctx", "tensor"), None),
        P("tensor"),
        P("tensor"),
    )
    out_specs = P(("ctx", "tensor"), None)
    return jax.shard_map(
        exchange, mesh=mesh, in_specs=in_specs, out_specs=out_specs, check_vma=False
    )
```

```python
import jax
import jax.numpy as jnp
from jax import lax
from jax.experimental import pallas as pl
from jax.experimental.pallas import tpu as pltpu
from jax.sharding import PartitionSpec as P

HEADS = 32
KV_HEADS = 8
HEAD_DIM = 128
RATE_MID = 8
RATE_FAR = 64


NEG_FILL = -1e30


RING = 8
MESH_IDS = pl.DeviceIdType.MESH


CHUNK = 128


def exchange_body(
    q_ref, key_ref, value_ref, mid_off, far_off,
    result,
    kv_ref, mid_ref, fk_ref, fv_ref,
    q_out, prev_out, mid_out, fk_out, fv_out, near_out, max_out, sum_out, staged,
    local_sem, prev_send, prev_recv, q_send, q_recv, x_send, x_recv,
    mid_send, mid_recv, fwd_send, fwd_recv,
    k1_send, k1_recv, v1_send, v1_recv, k2_send, k2_recv, v2_send, v2_recv,
    back_send, back_recv, kv_send, kv_recv,
):
    place = lax.axis_index("ctx")
    lane = lax.axis_index("tensor")
    total = 2 * RING * RING
    lanes = q_out.shape[0]
    width = q_out.shape[2]
    kv_local = kv_ref.shape[1] // (2 * HEAD_DIM)
    per_group = width // (kv_local * HEAD_DIM)
    z = lax.rem(place, RING)
    y = lax.rem(place // RING, RING)
    x = place // (RING * RING)

    def at(xi, yi, zi):
        return {"ctx": (xi * RING + yi) * RING + zi}

    def z_peer(step):
        return at(x, y, lax.rem(z + RING + step, RING))

    def y_peer(step):
        return at(x, lax.rem(y + RING + step, RING), z)

    x_peer = at(1 - x, y, z)
    parity = lax.rem(y, 2)
    y_pair = at(x, y + 1 - 2 * parity, z)
    after = {"ctx": lax.rem(place + 1, total)}
    before = {"ctx": lax.rem(place + total - 1, total)}

    barrier = pltpu.get_barrier_semaphore()
    greeted = [x_peer, after, before]
    greeted += [z_peer(step) for step in range(1, RING)]
    greeted += [y_peer(step) for step in range(1, RING)]
    greeted += [{"tensor": lax.rem(lane + step, lanes)} for step in range(1, lanes)]
    for peer in greeted:
        pl.semaphore_signal(barrier, inc=1, device_id=peer, device_id_type=MESH_IDS)
    pl.semaphore_wait(barrier, len(greeted))

    def remote(source, target, send, recv, peer):
        copy = pltpu.make_async_remote_copy(
            src_ref=source, dst_ref=target, send_sem=send, recv_sem=recv,
            device_id=peer, device_id_type=MESH_IDS,
        )
        copy.start()
        return copy

    def columns(index):
        return pl.ds(pl.multiple_of(index * width, width), width)

    class Ring:
        def __init__(self, block, place_in, peer, send, recv, own, hops):
            self.block, self.place, self.peer = block, place_in, peer
            self.send, self.recv, self.own, self.hops = send, recv, own, hops
            self.sent = {}

        def source(self, way, step):
            return lax.rem(self.place + 2 * RING - way * step, RING)

        def start(self, step):
            for slot, way in ((0, 1), (1, -1)):
                if step > self.hops[slot]:
                    continue
                target = self.block(self.source(way, step - 1))
                origin = target
                if step == 1 and self.own is not None:
                    origin = self.own
                index = slot * RING + step
                self.sent[slot, step] = remote(
                    origin, target, self.send.at[index], self.recv.at[index], self.peer(way)
                )

        def landed(self, step):
            found = []
            for slot, way in ((0, 1), (1, -1)):
                if step <= self.hops[slot]:
                    self.sent[slot, step].wait_recv()
                    found.append((slot * RING + step, self.block(self.source(way, step))))
            return found

        def finish(self):
            for copy in self.sent.values():
                copy.wait_send()

    tokens, kv_wide = kv_ref.shape
    half = kv_wide // 2
    mine_rows = pl.ds(pl.multiple_of(lane * CHUNK, CHUNK), CHUNK)

    def kv_columns(index):
        return pl.ds(pl.multiple_of(index * half, half), half)

    shares = []
    for part, source in enumerate((key_ref, value_ref)):
        target = kv_ref.at[mine_rows, pl.ds(part * half, half)]
        own_part = pltpu.make_async_copy(
            source.at[:, kv_columns(lane)], target, local_sem.at[5 + part]
        )
        own_part.start()
        shares.append((own_part, target))
    arriving = []
    for step in (2, 1, 3):
        other = lax.rem(lane + step, lanes)
        for part, source in enumerate((key_ref, value_ref)):
            arriving.append(
                remote(
                    source.at[:, kv_columns(other)], shares[part][1],
                    kv_send.at[part, step], kv_recv.at[part, step], {"tensor": other},
                )
            )
    own_q = pltpu.make_async_copy(q_ref.at[:, columns(lane)], q_out.at[lane], local_sem.at[3])
    own_q.start()
    moves = []
    for step in range(1, lanes):
        other = lax.rem(lane + step, lanes)
        moves.append(
            remote(
                q_ref.at[:, columns(other)], q_out.at[lane],
                q_send.at[step], q_recv.at[step], {"tensor": other},
            )
        )
    for own_part, _ in shares:
        own_part.wait()
    for copy in arriving:
        copy.wait_recv()

    def one_hot(offset, rate):
        count = tokens // rate
        row = lax.broadcasted_iota(jnp.int32, (count, tokens), 0)
        col = lax.broadcasted_iota(jnp.int32, (count, tokens), 1)
        return jnp.where(col == row * rate + offset, 1.0, 0.0).astype(jnp.bfloat16)

    mid_hot = [one_hot(mid_off[head], RATE_MID) for head in range(kv_local)]
    far_hot = [one_hot(far_off[head], RATE_FAR) for head in range(kv_local)]
    far_rows = []
    for part in range(2):
        for head in range(kv_local):
            cols = slice((part * kv_local + head) * HEAD_DIM, (part * kv_local + head + 1) * HEAD_DIM)
            block = kv_ref[:, cols]
            mid_ref[:, cols] = jnp.dot(
                mid_hot[head], block, preferred_element_type=jnp.float32
            ).astype(jnp.bfloat16)
            far_rows.append(
                jnp.dot(far_hot[head], block, preferred_element_type=jnp.float32)
            )
    fk_ref[...] = jnp.concatenate(far_rows[:kv_local], 0).astype(jnp.bfloat16)
    fv_ref[...] = jnp.concatenate(far_rows[kv_local:], 0).astype(jnp.bfloat16)

    own_mid = pltpu.make_async_copy(mid_ref, mid_out.at[parity, z], local_sem.at[2])
    own_mid.start()
    mid_ring = Ring(
        lambda i: mid_out.at[parity, i], z, z_peer, mid_send, mid_recv, mid_ref, (3, 4)
    )
    mid_ring.start(1)
    forwards = [
        remote(mid_ref, mid_out.at[parity, z], fwd_send.at[0], fwd_recv.at[0], y_pair)
    ]
    own_k = pltpu.make_async_copy(fk_ref, fk_out.at[y, z, x], local_sem.at[0])
    own_v = pltpu.make_async_copy(fv_ref, fv_out.at[z, y, x], local_sem.at[1])
    own_k.start()
    own_v.start()
    x_k = remote(fk_ref, fk_out.at[y, z, x], x_send.at[0], x_recv.at[0], x_peer)
    x_v = remote(fv_ref, fv_out.at[z, y, x], x_send.at[1], x_recv.at[1], x_peer)
    ahead = {}

    def pass_on(chunk):
        rows = pl.ds(chunk * CHUNK, CHUNK)
        ahead[chunk] = remote(
            kv_ref.at[rows], prev_out.at[rows], prev_send.at[chunk], prev_recv.at[chunk], after
        )

    order = [4, 3, 5, 2, 6, 1, 7]
    pass_on(3)
    own_k.wait()
    own_v.wait()
    x_k.wait_recv()
    x_v.wait_recv()
    firsts_k = {
        step: remote(
            fk_out.at[y, z], fk_out.at[y, z], k1_send.at[step], k1_recv.at[step], z_peer(step)
        )
        for step in order
    }
    firsts_v = {
        step: remote(
            fv_out.at[z, y], fv_out.at[z, y], v1_send.at[step], v1_recv.at[step], y_peer(step)
        )
        for step in order
    }

    def mid_step(step):
        found = mid_ring.landed(step - 1)
        if step <= 4:
            mid_ring.start(step)
        return found

    def forward(found):
        for index, block in found:
            forwards.append(
                remote(block, block, fwd_send.at[index], fwd_recv.at[index], y_pair)
            )

    found = mid_step(2)
    pass_on(2)
    for step in order:
        firsts_k[step].wait_recv()
        firsts_v[step].wait_recv()
    k_ring = Ring(lambda i: fk_out.at[i], y, y_peer, k2_send, k2_recv, None, (3, 4))
    v_ring = Ring(lambda i: fv_out.at[i], z, z_peer, v2_send, v2_recv, None, (3, 4))
    k_ring.start(1)
    v_ring.start(1)
    forward(found)

    def near(chunk):
        first = chunk * CHUNK
        span = kv_ref.shape[0] + CHUNK
        row = lax.broadcasted_iota(jnp.int32, (CHUNK, span), 0)
        col = lax.broadcasted_iota(jnp.int32, (CHUNK, span), 1)
        allowed = (col > row) & (col <= row + kv_ref.shape[0])
        allowed = allowed & ((col >= kv_ref.shape[0] - first) | (place > 0))
        bias = jnp.where(allowed, 0.0, NEG_FILL)
        bias = jnp.concatenate([bias] * per_group, 0)

        @pl.loop(0, kv_local)
        def _(head):
            def window(part):
                cols = pl.ds(
                    pl.multiple_of((part * kv_local + head) * HEAD_DIM, HEAD_DIM), HEAD_DIM
                )
                return jnp.concatenate(
                    [prev_out[first:, cols], kv_ref[: first + CHUNK, cols]], 0
                )

            group = per_group * HEAD_DIM
            wide = q_out[chunk, :, pl.ds(pl.multiple_of(head * group, group), group)]
            rows = jnp.concatenate(
                [wide[:, g * HEAD_DIM : (g + 1) * HEAD_DIM] for g in range(per_group)], 0
            )
            scores = lax.dot_general(
                rows, window(0), (((1,), (1,)), ((), ())), preferred_element_type=jnp.float32
            )
            scores = scores * HEAD_DIM ** (-0.5) + bias
            maxima = jnp.max(scores, axis=1, keepdims=True)
            powers = jnp.exp(scores - maxima)
            totals = jnp.sum(powers, axis=1, keepdims=True)
            weighted = jnp.dot(
                powers.astype(jnp.bfloat16), window(1), preferred_element_type=jnp.float32
            )
            for g in range(per_group):
                mine = slice(g * CHUNK, (g + 1) * CHUNK)
                near_out[head * per_group + g, first : first + CHUNK] = weighted[mine]
                max_out[head * per_group + g, first : first + CHUNK] = maxima[mine]
                sum_out[head * per_group + g, first : first + CHUNK] = totals[mine]

    found = mid_step(3)
    pass_on(1)
    own_q.wait()
    for copy in moves:
        copy.wait_recv()
    k_ring.landed(1)
    k_ring.start(2)
    v_ring.landed(1)
    v_ring.start(2)
    forward(found)
    pass_on(0)
    ahead[3].wait_recv()
    near(3)
    found = mid_step(4)
    k_ring.landed(2)
    k_ring.start(3)
    v_ring.landed(2)
    v_ring.start(3)
    forward(found)
    ahead[2].wait_recv()
    near(2)
    found = mid_step(5)
    k_ring.landed(3)
    k_ring.start(4)
    v_ring.landed(3)
    v_ring.start(4)
    forward(found)
    ahead[1].wait_recv()
    near(1)
    ahead[0].wait_recv()
    near(0)
    own_mid.wait()
    for copy in forwards:
        copy.wait_recv()
    group = per_group * HEAD_DIM

    def picked(head, chosen):
        wide = q_out[:, :, head * group : (head + 1) * group].reshape(tokens, group)
        rows = jnp.dot(chosen, wide, preferred_element_type=jnp.float32)
        parts = [rows[:, g * HEAD_DIM : (g + 1) * HEAD_DIM] for g in range(per_group)]
        return jnp.concatenate(parts, 0).astype(jnp.bfloat16)

    def attend(rows, key_rows, value_rows, bias):
        scores = lax.dot_general(
            rows, key_rows, (((1,), (1,)), ((), ())), preferred_element_type=jnp.float32
        )
        scores = scores * HEAD_DIM ** (-0.5) + jnp.concatenate([bias] * per_group, 0)
        maxima = jnp.max(scores, axis=1, keepdims=True)
        powers = jnp.exp(scores - maxima)
        totals = jnp.sum(powers, axis=1, keepdims=True)
        weighted = jnp.dot(
            powers.astype(jnp.bfloat16), value_rows, preferred_element_type=jnp.float32
        )
        return maxima, totals, weighted

    def mid_stats(head):
        count = tokens // RATE_MID
        span = 2 * RING * count
        row = lax.broadcasted_iota(jnp.int32, (count, span), 0)
        col = lax.broadcasted_iota(jnp.int32, (count, span), 1)
        bias = jnp.where(col <= lax.rem(place, 2 * RING) * count + row, 0.0, NEG_FILL)
        first = head * HEAD_DIM
        second = (kv_local + head) * HEAD_DIM
        return attend(
            picked(head, mid_hot[head]),
            mid_out[:, :, :, first : first + HEAD_DIM].reshape(span, HEAD_DIM),
            mid_out[:, :, :, second : second + HEAD_DIM].reshape(span, HEAD_DIM),
            bias,
        )

    mids = [mid_stats(head) for head in range(kv_local)]
    k_ring.landed(4)
    v_ring.landed(4)

    def far_stats(head):
        count = tokens // RATE_FAR
        span = total * kv_local * count
        row = lax.broadcasted_iota(jnp.int32, (count, span), 0)
        col = lax.broadcasted_iota(jnp.int32, (count, span), 1)
        inner = lax.rem(col, count)
        owner = lax.rem(col // count, kv_local)
        block = col // (count * kv_local)
        source = lax.rem(block, 2) * (RING * RING) + block // 2
        allowed = (owner == head) & (source * count + inner <= place * count + row)
        key_rows = fk_out[...].reshape(span, HEAD_DIM)
        value_rows = jnp.concatenate(
            [fv_out[:, i].reshape(span // RING, HEAD_DIM) for i in range(RING)], 0
        )
        return attend(
            picked(head, far_hot[head]),
            key_rows, value_rows, jnp.where(allowed, 0.0, NEG_FILL),
        )

    fars = [far_stats(head) for head in range(kv_local)]
    token = lax.broadcasted_iota(jnp.int32, (tokens, HEAD_DIM), 0)

    def spread(stats, head, g, offset, rate):
        count = tokens // rate
        full = []
        for part in stats:
            part = jnp.broadcast_to(part[g * count : (g + 1) * count], (count, HEAD_DIM))
            part = jnp.broadcast_to(part[:, None, :], (count, rate, HEAD_DIM))
            full.append(part.reshape(tokens, HEAD_DIM))
        full[0] = jnp.where(lax.rem(token, rate) == offset, full[0], NEG_FILL)
        return full

    def send_back(head):
        for step in range(1, lanes):
            other = lax.rem(lane + step, lanes)
            start = pl.multiple_of(lane * width + head * group, group)
            backs.append(
                remote(
                    staged.at[other, :, pl.ds(head * group, group)],
                    result.at[:, pl.ds(start, group)],
                    back_send.at[head, step], back_recv.at[head, step], {"tensor": other},
                )
            )

    backs = []
    for head in range(kv_local):
        for g in range(per_group):
            index = head * per_group + g
            near_parts = (
                jnp.broadcast_to(max_out[index], (tokens, HEAD_DIM)),
                jnp.broadcast_to(sum_out[index], (tokens, HEAD_DIM)),
                near_out[index],
            )
            branches = (
                near_parts,
                spread(mids[head], head, g, mid_off[head], RATE_MID),
                spread(fars[head], head, g, far_off[head], RATE_FAR),
            )
            highest = jnp.maximum(
                jnp.maximum(branches[0][0], branches[1][0]), branches[2][0]
            )
            numerator = jnp.zeros((tokens, HEAD_DIM), jnp.float32)
            denominator = jnp.zeros((tokens, HEAD_DIM), jnp.float32)
            for maxima, totals, weighted in branches:
                factor = jnp.exp(maxima - highest)
                denominator = denominator + factor * totals
                numerator = numerator + factor * weighted
            attended = (numerator / denominator).astype(jnp.bfloat16)
            staged[:, :, index * HEAD_DIM : (index + 1) * HEAD_DIM] = attended.reshape(
                lanes, tokens // lanes, HEAD_DIM
            )
            if head > 0 and g == 0:
                send_back(head - 1)
    send_back(kv_local - 1)
    own_back = pltpu.make_async_copy(
        staged.at[lane], result.at[:, columns(lane)], local_sem.at[4]
    )
    own_back.start()
    x_k.wait_send()
    x_v.wait_send()
    for step in order:
        firsts_k[step].wait_send()
        firsts_v[step].wait_send()
    for copy in arriving + forwards + moves + list(ahead.values()):
        copy.wait_send()
    for ring in (mid_ring, k_ring, v_ring):
        ring.finish()
    own_back.wait()
    for copy in backs:
        copy.wait()


def exchange(queries, keys, values, mid_offsets, far_offsets):
    lanes = lax.axis_size("tensor")
    own, wide = queries.shape
    rows = own * lanes
    heads = HEADS // lanes
    kv_local = mid_offsets.shape[0]
    kv_shape = (rows, 2 * kv_local * HEAD_DIM)
    mid_shape = (rows // RATE_MID, kv_shape[1])
    far_shape = (kv_local * rows // RATE_FAR, HEAD_DIM)
    sizes = [7, 4, 4, 4, 4, 2, 2] + [2 * RING] * 12
    vmem = pl.BlockSpec(memory_space=pltpu.VMEM)
    smem = pl.BlockSpec(memory_space=pltpu.SMEM)
    return pl.pallas_call(
        exchange_body,
        out_shape=jax.ShapeDtypeStruct((own, wide), jnp.bfloat16),
        in_specs=[vmem] * 3 + [smem] * 2,
        out_specs=vmem,
        scratch_shapes=[
            pltpu.VMEM(kv_shape, jnp.bfloat16),
            pltpu.VMEM(mid_shape, jnp.bfloat16),
            pltpu.VMEM(far_shape, jnp.bfloat16),
            pltpu.VMEM(far_shape, jnp.bfloat16),
            pltpu.VMEM((lanes, own, wide // lanes), jnp.bfloat16),
            pltpu.VMEM(kv_shape, jnp.bfloat16),
            pltpu.VMEM((2, RING) + mid_shape, jnp.bfloat16),
            pltpu.VMEM((RING, RING, 2) + far_shape, jnp.bfloat16),
            pltpu.VMEM((RING, RING, 2) + far_shape, jnp.bfloat16),
            pltpu.VMEM((heads, rows, HEAD_DIM), jnp.float32),
            pltpu.VMEM((heads, rows, 1), jnp.float32),
            pltpu.VMEM((heads, rows, 1), jnp.float32),
            pltpu.VMEM((lanes, own, wide // lanes), jnp.bfloat16),
        ]
        + [pltpu.SemaphoreType.DMA((size,)) for size in sizes]
        + [pltpu.SemaphoreType.DMA((kv_local, lanes))] * 2
        + [pltpu.SemaphoreType.DMA((2, lanes))] * 2,
        compiler_params=pltpu.CompilerParams(
            collective_id=0, has_side_effects=True, vmem_limit_bytes=56 * 2**20
        ),
        name="exchange",
    )(queries, keys, values, mid_offsets, far_offsets)


def solution(mesh):
    in_specs = (
        P(("ctx", "tensor"), None),
        P(("ctx", "tensor"), None),
        P(("ctx", "tensor"), None),
        P("tensor"),
        P("tensor"),
    )
    out_specs = P(("ctx", "tensor"), None)
    return jax.shard_map(
        exchange, mesh=mesh, in_specs=in_specs, out_specs=out_specs, check_vma=False
    )
```
